32 devices in a mesh: tm: 4 (over y, x), space: 8 (over z, core).
Axes of the slice: x: 2, y: 2, z: 4, core: 2. Of those that a mesh axis runs over, the one named last changes fastest.
Arguments:
- starts: float32 [4, 3, 64, 64, 128], P('tm', None, 'space'), may hold values from -6 to 6
- strain: bfloat16 [4, 9, 64, 64, 128], P('tm', None, 'space'), may hold values from -0.59765625 to 0.59765625
Outputs:
- corrected: float32 [4, 3, 64, 64, 128], P('tm', None, 'space')
The draws below stay inside these ranges and needn't reach their ends.
All inputs are finite; a program needn't handle non-finite values.
Results may differ from the reference program's by a relative error of at most 0.0003.
Values sent between devices are 32-bit elements; how exact they have to be, the bound alone decides.
A program may use at most 128 MiB of HBM per device.

```python
import jax
import jax.numpy as jnp
from jax import lax

CX = 64
CY = 128
COARSEN = 4
SLICES = 4
NZ = 64


def block_levels(own_key, dims, pieces, low, high):
    loudness, own = 1.0, jax.random.fold_in(own_key, 6)
    for dim, parts in pieces:
        steps = jnp.exp(jax.random.uniform(jax.random.fold_in(own, dim), (parts,), jnp.float32, low / len(pieces), high / len(pieces)))
        loudness = loudness * jnp.repeat(steps, dims[dim] // parts).reshape([-1 if axis == dim else 1 for axis in range(len(dims))])
    return loudness


def normal_values(stream_key, extent, scale, reach, pieces=(), dtype=jnp.bfloat16):
    values = jax.random.normal(stream_key, extent, jnp.float32) * scale
    if len(pieces) > 0:
        values = block_levels(stream_key, extent, pieces, -0.22, 0.18) * values
    return jnp.clip(values, min=-reach, max=reach).astype(dtype)


def setup_inputs(seed: int = 0) -> dict:
    streams_of = jax.random.split(jax.random.key(seed), 3)
    starts = normal_values(streams_of[0], (SLICES, 3, NZ, CX, CY), 1.0, 6.0, ((0, 4), (2, 8)), jnp.float32)
    strain = normal_values(streams_of[1], (SLICES, 9, NZ, CX, CY), 0.1, 0.59765625, ((0, 4), (2, 8)))
    return {"starts": starts, "strain": strain}


kernel_near = 0.8
kernel_far = 0.2
diffusion = 0.08
coarse_rate = 0.1

def depth_terms(padded, field, depth):
    near_sum = padded[:, 3:3 + depth] + padded[:, 1:1 + depth] - 2.0 * field
    far_sum = padded[:, 4:4 + depth] + padded[:, 0:depth] - 2.0 * field
    return kernel_near * near_sum + kernel_far * far_sum

def plane_terms(field):
    total = jnp.zeros_like(field)
    for along in (2, 3):
        near_sum = jnp.roll(field, 1, along) + jnp.roll(field, -1, along) - 2.0 * field
        far_sum = jnp.roll(field, 2, along) + jnp.roll(field, -2, along) - 2.0 * field
        total = total + kernel_near * near_sum + kernel_far * far_sum
    return total

def stretch_terms(field, strain):
    result = []
    for row in range(3):
        acc = strain[3 * row].astype(jnp.float32) * field[0]
        acc = acc + strain[3 * row + 1].astype(jnp.float32) * field[1]
        acc = acc + strain[3 * row + 2].astype(jnp.float32) * field[2]
        result.append(acc)
    return jnp.stack(result, axis=0)

def fine_step(field, strain):
    depth = field.shape[1]
    padded = jnp.pad(field, ((0, 0), (2, 2), (0, 0), (0, 0)))
    return field + stretch_terms(field, strain) + diffusion * (depth_terms(padded, field, depth) + plane_terms(field))

def restrict_field(field):
    comps, depth, width_x, width_y = field.shape
    blocks = field.reshape(comps, depth // COARSEN, COARSEN, width_x // COARSEN, COARSEN, width_y // COARSEN, COARSEN)
    return jnp.mean(blocks, axis=(2, 4, 6))

def prolong_field(coarse):
    comps, depth, width_x, width_y = coarse.shape
    spread = jnp.broadcast_to(coarse[:, :, None, :, None, :, None], (comps, depth, COARSEN, width_x, COARSEN, width_y, COARSEN))
    return spread.reshape(comps, depth * COARSEN, width_x * COARSEN, width_y * COARSEN)

def coarse_step(field, padded):
    near_sum = padded[..., 2:, :, :] + padded[..., :-2, :, :]
    near_sum = near_sum + jnp.roll(field, 1, -2) + jnp.roll(field, -1, -2)
    near_sum = near_sum + jnp.roll(field, 1, -1) + jnp.roll(field, -1, -1)
    return field + coarse_rate * (near_sum - 6.0 * field)

def solve_small(factor, vector):
    lower = lax.linalg.triangular_solve(factor, vector[:, None], left_side=True, lower=True)
    upper = lax.linalg.triangular_solve(factor, lower, left_side=True, lower=True, transpose_a=True)
    return upper[:, 0]

def reference(starts, strain):
    count = starts.shape[0]
    fine_ends = lax.map(lambda inputs: fine_step(inputs[0], inputs[1]), (starts, strain))
    snap_basis = jnp.stack([restrict_field(starts[index]) for index in range(count)], axis=0)
    images = jnp.stack([restrict_field(fine_ends[index]) for index in range(count)], axis=0)
    flat_basis = snap_basis.reshape(count, -1)
    flat_images = images.reshape(count, -1)
    gram_matrix = jnp.dot(flat_basis, flat_basis.T, precision=lax.Precision.HIGHEST)
    factor = jnp.linalg.cholesky(gram_matrix)
    shape = snap_basis.shape[1:]

    def kapply(gap):
        product = jnp.dot(flat_basis, gap.reshape(-1), precision=lax.Precision.HIGHEST)
        coeffs = solve_small(factor, product)
        remainder = gap - jnp.dot(coeffs, flat_basis, precision=lax.Precision.HIGHEST).reshape(shape)
        padded = jnp.pad(remainder, ((0, 0), (1, 1), (0, 0), (0, 0)))
        return jnp.dot(coeffs, flat_images, precision=lax.Precision.HIGHEST).reshape(shape) + coarse_step(remainder, padded)
    gap = jnp.zeros(shape, jnp.float32)
    outputs = []
    for index in range(count):
        carried = kapply(gap)
        outputs.append(fine_ends[index] + prolong_field(carried))
        if index + 1 < count:
            gap = images[index] + carried - snap_basis[index + 1]
    return jnp.stack(outputs, axis=0)
```

```python
import functools

import jax
import jax.numpy as jnp
from jax import lax
from jax.experimental import pallas as pl
from jax.experimental.pallas import tpu as pltpu
from jax.sharding import PartitionSpec as P

COARSEN = 4
NEAR = 0.8
FAR = 0.2
DIFFUSION = 0.08
RATE = 0.1
LANES = 128
HI = lax.Precision.HIGHEST
MESH = pl.DeviceIdType.MESH


def iota(shape, dim):
    return lax.broadcasted_iota(jnp.int32, shape, dim)


def dot(a, b, dims=((1,), (0,))):
    return lax.dot_general(a, b, (dims, ((), ())), precision=HI, preferred_element_type=jnp.float32)


def pick(condition):
    return jnp.where(condition, 1.0, 0.0).astype(jnp.float32)


class Plan:
    def __init__(self, slices, slabs, block):
        self.S, self.Z = slices, slabs
        self.C, self.D, self.X, self.Y = block
        self.p = self.D // COARSEN
        self.nx, self.ny = self.X // COARSEN, self.Y // COARSEN
        self.groups = LANES // self.ny
        self.rp = self.nx // self.groups
        self.rows = self.p * self.rp
        self.H = min(slabs - 1, -(-(slices - 1) // self.p))
        self.W = 2 * self.H + 1
        self.N = slices * slabs
        self.count = 2 * (slices - 1) * slices
        self.LQ = -(-self.count // LANES) * LANES


def step_tools(plan):
    shape = (plan.rows, LANES)
    row, lane = iota(shape, 0), iota(shape, 1)
    low = row % plan.rp
    y = lane % plan.ny
    return dict(
        last_y=y == plan.ny - 1,
        first_y=y == 0,
        last_x=low == plan.rp - 1,
        first_x=low == 0,
        last_z=row >= plan.rows - plan.rp,
        first_z=row < plan.rp,
    )


def coarse_step(plan, tools, prev, cur, nxt):
    rows, rp, ny = plan.rows, plan.rp, plan.ny
    roll = pltpu.roll
    total = jnp.where(tools["last_y"], roll(cur, ny - 1, 1), roll(cur, LANES - 1, 1))
    total += jnp.where(tools["first_y"], roll(cur, LANES - ny + 1, 1), roll(cur, 1, 1))
    total += jnp.where(
        tools["last_x"], roll(roll(cur, rp - 1, 0), LANES - ny, 1), roll(cur, rows - 1, 0)
    )
    total += jnp.where(
        tools["first_x"], roll(roll(cur, rows - rp + 1, 0), ny, 1), roll(cur, 1, 0)
    )
    up = roll(cur, rows - rp, 0)
    down = roll(cur, rp, 0)
    zero = jnp.zeros_like(cur)
    above = zero if nxt is None else roll(nxt, rows - rp, 0)
    below = zero if prev is None else roll(prev, rp, 0)
    total += jnp.where(tools["last_z"], above, up) + jnp.where(tools["first_z"], below, down)
    return cur + RATE * (total - 6.0 * cur)


def kernel(
    plan, start_hbm, strain_hbm, fine_hbm, add_ref,
    f, st, o, bx, ix, prod, mbuf,
    in_sem, out_sem, halo_send, halo_recv, b_send, b_recv, i_send, i_recv, m_send, m_recv,
):
    S, Z, C, D, X, Y, H, W, N = (
        plan.S, plan.Z, plan.C, plan.D, plan.X, plan.Y, plan.H, plan.W, plan.N
    )
    p, rows, groups, rp, ny = plan.p, plan.rows, plan.groups, plan.rp, plan.ny
    t, s = lax.axis_index("tm"), lax.axis_index("space")
    me = s * S + t

    load_start = pltpu.make_async_copy(start_hbm.at[0], f.at[:, pl.ds(2, D)], in_sem.at[0])
    load_start.start()
    load_strain = pltpu.make_async_copy(strain_hbm.at[0], st, in_sem.at[1])
    load_strain.start()

    barrier = pltpu.get_barrier_semaphore()

    def greet(k, carry):
        peer = lax.rem(me + k, N)
        pl.semaphore_signal(
            barrier, inc=1, device_id=(lax.rem(peer, S), peer // S), device_id_type=MESH
        )
        return carry

    lax.fori_loop(1, N, greet, 0)

    spread_y = pick(iota((Y, LANES), 0) // COARSEN == iota((Y, LANES), 1) % ny)
    tall = (groups * rows, p * X)
    a, b = iota(tall, 0), iota(tall, 1)
    coarse_x = (a // rows) * rp + a % rp
    gather_x = pick(((a % rows) // rp == b // X) & ((b % X) // COARSEN == coarse_x))
    group_of = iota((rows, LANES), 1) // ny

    def restrict(plane_sums):
        wide = dot(jnp.concatenate(plane_sums, axis=0), spread_y)
        result = []
        for c in range(C):
            tallc = dot(gather_x, wide[c * p * X : (c + 1) * p * X])
            total = jnp.zeros((rows, LANES), jnp.float32)
            for g in range(groups):
                total += jnp.where(group_of == g, tallc[g * rows : (g + 1) * rows], 0.0)
            result.append(total * (1.0 / COARSEN**3))
        return result

    load_start.wait()
    sums = []
    for c in range(C):
        planes = []
        for zz in range(p):
            base = 2 + zz * COARSEN
            acc = f[c, base]
            for k in range(1, COARSEN):
                acc = acc + f[c, base + k]
            planes.append(acc)
        sums.append(jnp.concatenate(planes, axis=0))
    own_b = restrict(sums)
    for c in range(C):
        bx[H, t, c] = own_b[c]

    for d in range(-H, H + 1):
        if d != 0:

            @pl.when((s + d < 0) | (s + d >= Z))
            def _():
                bx[H + d] = jnp.zeros((S, C, rows, LANES), jnp.float32)
                ix[H + d] = jnp.zeros((S, C, rows, LANES), jnp.float32)

    @pl.when(s == 0)
    def _():
        f[:, 0:2] = jnp.zeros((C, 2, X, Y), jnp.float32)

    @pl.when(s == Z - 1)
    def _():
        f[:, D + 2 : D + 4] = jnp.zeros((C, 2, X, Y), jnp.float32)

    pl.semaphore_wait(barrier, N - 1)

    up_copy = pltpu.make_async_remote_copy(
        src_ref=f.at[:, pl.ds(D, 2)], dst_ref=f.at[:, pl.ds(0, 2)],
        send_sem=halo_send.at[0], recv_sem=halo_recv.at[0],
        device_id=(t, jnp.minimum(s + 1, Z - 1)), device_id_type=MESH,
    )
    down_copy = pltpu.make_async_remote_copy(
        src_ref=f.at[:, pl.ds(2, 2)], dst_ref=f.at[:, pl.ds(D + 2, 2)],
        send_sem=halo_send.at[1], recv_sem=halo_recv.at[1],
        device_id=(t, jnp.maximum(s - 1, 0)), device_id_type=MESH,
    )

    def share(buf, send, recv):
        order = sorted(range(-H, H + 1), key=abs)
        for d in order:

            def one(k, carry):
                pltpu.make_async_remote_copy(
                    src_ref=buf.at[H, t], dst_ref=buf.at[H - d, t],
                    send_sem=send.at[H + d], recv_sem=recv.at[H - d],
                    device_id=(lax.rem(t + k, S), s + d), device_id_type=MESH,
                ).start()
                return carry

            @pl.when((s + d >= 0) & (s + d < Z))
            def _():
                lax.fori_loop(1 if d == 0 else 0, S, one, 0)

    def settle(buf, sem):
        for d in range(-H, H + 1):
            size = S - 1 if d == 0 else S

            @pl.when((s + d >= 0) & (s + d < Z))
            def _():
                view = buf.at[H + d, pl.ds(0, size)]
                pltpu.make_async_copy(view, view, sem.at[H + d]).wait()

    share(bx, b_send, b_recv)

    @pl.when(s < Z - 1)
    def _():
        up_copy.start()

    @pl.when(s > 0)
    def _():
        down_copy.start()

    load_strain.wait()

    @pl.when(s > 0)
    def _():
        up_copy.wait_recv()

    @pl.when(s < Z - 1)
    def _():
        down_copy.wait_recv()

    near, far = DIFFUSION * NEAR, DIFFUSION * FAR
    centre = 1.0 - 6.0 * (near + far)

    def fine_plane(z, carry):
        v = [f[c, z + 2] for c in range(C)]
        for c in range(C):
            n1 = f[c, z + 1] + f[c, z + 3]
            n2 = f[c, z] + f[c, z + 4]
            n1 += pltpu.roll(v[c], 1, 0) + pltpu.roll(v[c], X - 1, 0)
            n2 += pltpu.roll(v[c], 2, 0) + pltpu.roll(v[c], X - 2, 0)
            n1 += pltpu.roll(v[c], 1, 1) + pltpu.roll(v[c], Y - 1, 1)
            n2 += pltpu.roll(v[c], 2, 1) + pltpu.roll(v[c], Y - 2, 1)
            acc = centre * v[c] + near * n1 + far * n2
            for j in range(C):
                acc += st[C * c + j, z].astype(jnp.float32) * v[j]
            o[c, z] = acc
        return carry

    lax.fori_loop(0, D, fine_plane, 0)
    store_fine = pltpu.make_async_copy(o, fine_hbm, out_sem)
    store_fine.start()

    sums = []
    for c in range(C):
        planes = []
        for zz in range(p):
            acc = o[c, zz * COARSEN]
            for k in range(1, COARSEN):
                acc = acc + o[c, zz * COARSEN + k]
            planes.append(acc)
        sums.append(jnp.concatenate(planes, axis=0))
    own_i = restrict(sums)
    for c in range(C):
        ix[H, t, c] = own_i[c]
    share(ix, i_send, i_recv)

    settle(bx, b_recv)
    tools = step_tools(plan)
    inside = [(s + d >= 0) & (s + d < Z) for d in range(-H, H + 1)]

    def advance(m_fields, reach):
        result = {}
        for d in range(-reach, reach + 1):
            out = coarse_step(plan, tools, m_fields.get(d - 1), m_fields[d], m_fields.get(d + 1))
            result[d] = out if d == 0 else jnp.where(inside[H + d], out, 0.0)
        return result

    prod[...] = jnp.zeros(prod.shape, jnp.float32)

    def powers(m, carry):
        sums_i = [None] * (S - 1)
        sums_b = [None] * (S - 1)
        for c in range(C):
            reach = min(H, -(-(S - 2) // p))
            fields = {d: bx[H + d, m, c] for d in range(-reach, reach + 1)}
            for k in range(S - 1):
                if k > 0:
                    fields = advance(fields, min(H, -(-(S - 2 - k) // p)))
                ti, tb = fields[0] * own_i[c], fields[0] * own_b[c]
                sums_i[k] = ti if c == 0 else sums_i[k] + ti
                sums_b[k] = tb if c == 0 else sums_b[k] + tb
        for k in range(S - 1):
            prod[k * S + m] = jnp.sum(sums_i[k], axis=0, keepdims=True)
            prod[(S - 1 + k) * S + m] = jnp.sum(sums_b[k], axis=0, keepdims=True)
        return carry

    if S <= 4:
        for m in range(S):
            powers(m, 0)
    else:
        lax.fori_loop(0, S, powers, 0)
    message = dot(jnp.ones((8, LANES), jnp.float32), prod[:, 0, :], ((1,), (1,)))
    mbuf[me] = message[0:1]

    def tell(k, carry):
        peer = lax.rem(me + k, N)
        pltpu.make_async_remote_copy(
            src_ref=mbuf.at[me], dst_ref=mbuf.at[me], send_sem=m_send, recv_sem=m_recv,
            device_id=(lax.rem(peer, S), peer // S), device_id_type=MESH,
        ).start()
        return carry

    lax.fori_loop(1, N, tell, 0)
    view = mbuf.at[pl.ds(0, N - 1)]
    pltpu.make_async_copy(view, view, m_recv).wait()
    owner = pick(iota((N, LANES), 0) % S == iota((N, LANES), 1))
    table = dot(mbuf[:, 0, :], owner, ((0,), (0,)))

    def block(kind, k):
        at = (kind * (S - 1) + k) * S
        return table[at : at + S]

    row, lane = iota((S, LANES), 0), iota((S, LANES), 1)
    lane1 = iota((1, LANES), 1)
    swept = block(1, 0)
    for i in range(S):
        pivot_row = swept[i : i + 1]
        pivot_col = jnp.sum(jnp.where(lane == i, swept, 0.0), axis=1, keepdims=True)
        pivot = jnp.sum(jnp.where(lane1 == i, pivot_row, 0.0), axis=1, keepdims=True)
        inv = 1.0 / pivot
        body = swept - pivot_col * (pivot_row * inv)
        body = jnp.where(row == i, pivot_row * inv, body)
        body = jnp.where(lane == i, pivot_col * inv, body)
        swept = jnp.where((row == i) & (lane == i), -inv, body)
    inverse = -swept
    mats = [block(0, k) - block(1, k + 1) for k in range(S - 2)]
    coeffs = []
    for j in range(1, S):
        p_col = jnp.sum(jnp.where(lane == 0, block(0, j - 1), 0.0), axis=1, keepdims=True)
        if j > 1:
            terms = jnp.zeros((S, LANES), jnp.float32)
            for i in range(1, j):
                terms += mats[j - 1 - i] * coeffs[i - 1]
            p_col = p_col + jnp.sum(terms, axis=1, keepdims=True)
        coeffs.append(
            jnp.where(lane1 < S, jnp.sum(inverse * p_col, axis=0, keepdims=True), 0.0)
        )

    settle(ix, i_recv)

    carried = []
    weights = [
        [jnp.sum(jnp.where(lane1 == m, coeffs[j], 0.0), axis=1, keepdims=True) for m in range(S)]
        for j in range(S - 1)
    ]
    for c in range(C):
        w = {d: ix[H + d, 0, c] for d in range(-H, H + 1)}
        mine = w[0]
        for j in range(1, S):
            reach = min(H, -(-(S - 1 - j) // p))
            source = min(H, reach + 1)
            left = {}
            for d in range(-source, source + 1):
                if d not in w:
                    continue
                value = w[d]
                for m in range(S):
                    value = value - weights[j - 1][m] * bx[H + d, m, c]
                left[d] = value
            moved = advance(left, reach)
            w = {}
            for d in range(-reach, reach + 1):
                value = moved[d]
                for m in range(S):
                    value = value + weights[j - 1][m] * ix[H + d, m, c]
                w[d] = value
            mine = jnp.where(t == j, w[0], mine)
        carried.append(mine - own_i[c])

    for c in range(C):
        stack = jnp.concatenate(
            [jnp.where(group_of == g, carried[c], 0.0) for g in range(groups)], axis=0
        )
        tallc = dot(gather_x, stack, ((0,), (0,)))
        full = dot(tallc, spread_y, ((1,), (1,)))
        for zz in range(p):
            add_ref[c, zz] = full[zz * X : (zz + 1) * X]

    store_fine.wait()
    settle(bx, b_send)
    settle(ix, i_send)
    pltpu.make_async_copy(view, view, m_send).wait()

    @pl.when(s < Z - 1)
    def _():
        up_copy.wait_send()

    @pl.when(s > 0)
    def _():
        down_copy.wait_send()


def local(starts, strain):
    slices, slabs = lax.axis_size("tm"), lax.axis_size("space")
    plan = Plan(slices, slabs, starts.shape[1:])
    C, D, X, Y = starts.shape[1:]
    f32 = jnp.float32
    coarse = (plan.W, plan.S, C, plan.rows, LANES)
    dma = pltpu.SemaphoreType.DMA
    fine, add = pl.pallas_call(
        functools.partial(kernel, plan),
        out_shape=(
            jax.ShapeDtypeStruct((C, D, X, Y), f32),
            jax.ShapeDtypeStruct((C, plan.p, X, Y), f32),
        ),
        in_specs=[pl.BlockSpec(memory_space=pl.ANY)] * 2,
        out_specs=(
            pl.BlockSpec(memory_space=pl.ANY),
            pl.BlockSpec(memory_space=pltpu.VMEM),
        ),
        scratch_shapes=[
            pltpu.VMEM((C, D + 4, X, Y), f32),
            pltpu.VMEM(strain.shape[1:], strain.dtype),
            pltpu.VMEM((C, D, X, Y), f32),
            pltpu.VMEM(coarse, f32),
            pltpu.VMEM(coarse, f32),
            pltpu.VMEM((plan.LQ, 1, LANES), f32),
            pltpu.VMEM((plan.N, 1, plan.LQ), f32),
            dma((2,)), dma(()), dma((2,)), dma((2,)),
            dma((plan.W,)), dma((plan.W,)), dma((plan.W,)), dma((plan.W,)),
            dma(()), dma(()),
        ],
        compiler_params=pltpu.CompilerParams(collective_id=0, has_side_effects=True),
    )(starts, strain)
    shape = (C, plan.p, COARSEN, X, Y)
    return (fine.reshape(shape) + add[:, :, None]).reshape(1, C, D, X, Y)


def solution(mesh):
    return jax.shard_map(
        local,
        mesh=mesh,
        in_specs=(P("tm", None, "space", None, None), P("tm", None, "space", None, None)),
        out_specs=P("tm", None, "space", None, None),
        check_vma=False,
    )
```

```python
import functools

import jax
import jax.numpy as jnp
from jax import lax
from jax.experimental import pallas as pl
from jax.experimental.pallas import tpu as pltpu
from jax.sharding import PartitionSpec as P

COARSEN = 4
NEAR = 0.8
FAR = 0.2
DIFFUSION = 0.08
RATE = 0.1
LANES = 128
HI = lax.Precision.HIGHEST
MESH = pl.DeviceIdType.MESH


def iota(shape, dim):
    return lax.broadcasted_iota(jnp.int32, shape, dim)


def dot(a, b, dims=((1,), (0,))):
    return lax.dot_general(a, b, (dims, ((), ())), precision=HI, preferred_element_type=jnp.float32)


def pick(condition):
    return jnp.where(condition, 1.0, 0.0).astype(jnp.float32)


class Plan:
    def __init__(self, slices, slabs, block):
        self.S, self.Z = slices, slabs
        self.C, self.D, self.X, self.Y = block
        self.p = self.D // COARSEN
        self.nx, self.ny = self.X // COARSEN, self.Y // COARSEN
        self.groups = LANES // self.ny
        self.rp = self.nx // self.groups
        self.rows = self.p * self.rp
        self.H = min(slabs - 1, -(-(slices - 1) // self.p))
        self.W = 2 * self.H + 1
        self.R = min(self.H, -(-(slices - 2) // self.p))
        self.SP = -(-slices // 8) * 8
        self.count = 2 * (slices - 1) * slices
        self.LQ = -(-self.count // LANES) * LANES


def step_tools(plan):
    shape = (plan.rows, LANES)
    row, lane = iota(shape, 0), iota(shape, 1)
    low = row % plan.rp
    y = lane % plan.ny
    return dict(
        last_y=y == plan.ny - 1,
        first_y=y == 0,
        last_x=low == plan.rp - 1,
        first_x=low == 0,
        last_z=row >= plan.rows - plan.rp,
        first_z=row < plan.rp,
    )


def coarse_step(plan, tools, prev, cur, nxt):
    rows, rp, ny = plan.rows, plan.rp, plan.ny
    roll = pltpu.roll
    total = jnp.where(tools["last_y"], roll(cur, ny - 1, 1), roll(cur, LANES - 1, 1))
    total += jnp.where(tools["first_y"], roll(cur, LANES - ny + 1, 1), roll(cur, 1, 1))
    total += jnp.where(
        tools["last_x"], roll(roll(cur, rp - 1, 0), LANES - ny, 1), roll(cur, rows - 1, 0)
    )
    total += jnp.where(
        tools["first_x"], roll(roll(cur, rows - rp + 1, 0), ny, 1), roll(cur, 1, 0)
    )
    up = roll(cur, rows - rp, 0)
    down = roll(cur, rp, 0)
    zero = jnp.zeros_like(cur)
    above = zero if nxt is None else roll(nxt, rows - rp, 0)
    below = zero if prev is None else roll(prev, rp, 0)
    total += jnp.where(tools["last_z"], above, up) + jnp.where(tools["first_z"], below, down)
    return cur + RATE * (total - 6.0 * cur)


def kernel(
    plan, start_hbm, strain_hbm, fine_hbm, add_ref,
    f, st, o, lo, hi, eb, bx, ix, prod, mz, mt,
    in_sem, out_sem, halo_send, halo_recv, e_send, e_recv,
    b_send, b_recv, i_send, i_recv, m_send, m_recv,
):
    S, Z, C, D, X, Y, H, R = (
        plan.S, plan.Z, plan.C, plan.D, plan.X, plan.Y, plan.H, plan.R
    )
    p, rows, groups, rp, ny = plan.p, plan.rows, plan.groups, plan.rp, plan.ny
    t, s = lax.axis_index("tm"), lax.axis_index("space")

    load_start = pltpu.make_async_copy(start_hbm.at[0], f.at[:, pl.ds(2, D)], in_sem.at[0])
    load_start.start()
    load_strain = pltpu.make_async_copy(strain_hbm.at[0], st, in_sem.at[1])
    load_strain.start()

    barrier = pltpu.get_barrier_semaphore()

    def greet_slices(slab, first):
        def one(k, carry):
            pl.semaphore_signal(
                barrier, inc=1, device_id=(lax.rem(t + k, S), slab), device_id_type=MESH
            )
            return carry

        lax.fori_loop(first, S, one, 0)

    def greet_slab(slab, carry):
        near = (slab - s <= H) & (s - slab <= H)

        @pl.when(near & (slab != s))
        def _():
            greet_slices(slab, 0)

        @pl.when(jnp.logical_not(near))
        def _():
            pl.semaphore_signal(barrier, inc=1, device_id=(t, slab), device_id_type=MESH)

        return carry

    greet_slices(s, 1)
    lax.fori_loop(0, Z, greet_slab, 0)
    near_slabs = jnp.minimum(s + H, Z - 1) - jnp.maximum(s - H, 0) + 1
    greetings = near_slabs * S - 1 + Z - near_slabs

    spread_y = pick(iota((Y, LANES), 0) // COARSEN == iota((Y, LANES), 1) % ny)
    tall = (groups * rows, p * X)
    a, b = iota(tall, 0), iota(tall, 1)
    coarse_x = (a // rows) * rp + a % rp
    gather_x = pick(((a % rows) // rp == b // X) & ((b % X) // COARSEN == coarse_x))
    group_of = iota((rows, LANES), 1) // ny

    def restrict(plane_sums):
        wide = dot(jnp.concatenate(plane_sums, axis=0), spread_y)
        result = []
        for c in range(len(plane_sums)):
            tallc = dot(gather_x, wide[c * p * X : (c + 1) * p * X])
            total = jnp.zeros((rows, LANES), jnp.float32)
            for g in range(groups):
                total += jnp.where(group_of == g, tallc[g * rows : (g + 1) * rows], 0.0)
            result.append(total * (1.0 / COARSEN**3))
        return result

    load_start.wait()
    sums = []
    for c in range(C):
        planes = []
        for zz in range(p):
            base = 2 + zz * COARSEN
            acc = f[c, base]
            for k in range(1, COARSEN):
                acc = acc + f[c, base + k]
            planes.append(acc)
        sums.append(jnp.concatenate(planes, axis=0))
    for c in range(C):
        bottom = (NEAR + FAR) * f[c, 2] + FAR * f[c, 3]
        top = (NEAR + FAR) * f[c, D + 1] + FAR * f[c, D]
        middle = [jnp.zeros((X, Y), jnp.float32)] * (p - 2)
        sums.append(jnp.concatenate([bottom] + middle + [top], axis=0))
    both = restrict(sums)
    own_b, own_e = both[:C], both[C:]
    for c in range(C):
        bx[H, t, c] = own_b[c]
        eb[0, c] = own_e[c]

    for d in range(-H, H + 1):
        if d != 0:

            @pl.when((s + d < 0) | (s + d >= Z))
            def _():
                bx[H + d] = jnp.zeros((S, C, rows, LANES), jnp.float32)
                ix[H + d] = jnp.zeros((S, C, rows, LANES), jnp.float32)

    f[:, 0:2] = jnp.zeros((C, 2, X, Y), jnp.float32)
    f[:, D + 2 : D + 4] = jnp.zeros((C, 2, X, Y), jnp.float32)

    @pl.when(s == 0)
    def _():
        lo[...] = jnp.zeros((C, 2, X, Y), jnp.float32)
        eb[1] = jnp.zeros((C, rows, LANES), jnp.float32)

    @pl.when(s == Z - 1)
    def _():
        hi[...] = jnp.zeros((C, 2, X, Y), jnp.float32)
        eb[2] = jnp.zeros((C, rows, LANES), jnp.float32)

    pl.semaphore_wait(barrier, greetings)

    above, below = (t, jnp.minimum(s + 1, Z - 1)), (t, jnp.maximum(s - 1, 0))

    def send(src, dst, send_sem, recv_sem, device):
        return pltpu.make_async_remote_copy(
            src_ref=src, dst_ref=dst, send_sem=send_sem, recv_sem=recv_sem,
            device_id=device, device_id_type=MESH,
        )

    halo_up = send(f.at[:, pl.ds(D, 2)], lo, halo_send.at[0], halo_recv.at[0], above)
    halo_down = send(f.at[:, pl.ds(2, 2)], hi, halo_send.at[1], halo_recv.at[1], below)
    edge_up = send(eb.at[0], eb.at[1], e_send.at[0], e_recv.at[0], above)
    edge_down = send(eb.at[0], eb.at[2], e_send.at[1], e_recv.at[1], below)

    def at_up(*actions):
        @pl.when(s < Z - 1)
        def _():
            for action in actions:
                action()

    def at_down(*actions):
        @pl.when(s > 0)
        def _():
            for action in actions:
                action()

    near_order = sorted(range(-R, R + 1), key=abs)
    far_order = [d for d in range(-H, H + 1) if abs(d) > R]

    def share(buf, send_sem, recv_sem, order, condition=True):
        for d in order:

            def one(k, carry):
                send(
                    buf.at[H, t], buf.at[H - d, t], send_sem.at[H + d], recv_sem.at[H - d],
                    (lax.rem(t + k, S), s + d),
                ).start()
                return carry

            @pl.when((s + d >= 0) & (s + d < Z) & condition)
            def _():
                lax.fori_loop(1 if d == 0 else 0, S, one, 0)

    def settle(buf, sem, order, size=S, condition=True):
        for d in order:

            @pl.when((s + d >= 0) & (s + d < Z) & condition)
            def _():
                view = buf.at[H + d, pl.ds(0, size - 1 if d == 0 else size)]
                pltpu.make_async_copy(view, view, sem.at[H + d]).wait()

    at_up(edge_up.start)
    at_down(edge_down.start)
    share(bx, b_send, b_recv, near_order)
    at_up(halo_up.start)
    at_down(halo_down.start)
    share(bx, b_send, b_recv, far_order)
    load_strain.wait()

    near, far = DIFFUSION * NEAR, DIFFUSION * FAR
    centre = 1.0 - 6.0 * (near + far)

    def fine_plane(z, carry):
        v = [f[c, z + 2] for c in range(C)]
        for c in range(C):
            n1 = f[c, z + 1] + f[c, z + 3]
            n2 = f[c, z] + f[c, z + 4]
            n1 += pltpu.roll(v[c], 1, 0) + pltpu.roll(v[c], X - 1, 0)
            n2 += pltpu.roll(v[c], 2, 0) + pltpu.roll(v[c], X - 2, 0)
            n1 += pltpu.roll(v[c], 1, 1) + pltpu.roll(v[c], Y - 1, 1)
            n2 += pltpu.roll(v[c], 2, 1) + pltpu.roll(v[c], Y - 2, 1)
            acc = centre * v[c] + near * n1 + far * n2
            for j in range(C):
                acc += st[C * c + j, z].astype(jnp.float32) * v[j]
            o[c, z // COARSEN, z % COARSEN] = acc
        return carry

    lax.fori_loop(0, D, fine_plane, 0)
    sums = []
    for c in range(C):
        planes = []
        for zz in range(p):
            acc = o[c, zz, 0]
            for k in range(1, COARSEN):
                acc = acc + o[c, zz, k]
            planes.append(acc)
        sums.append(jnp.concatenate(planes, axis=0))
    own_i = restrict(sums)
    tools = step_tools(plan)
    at_down(edge_up.wait_recv)
    at_up(edge_down.wait_recv)
    for c in range(C):
        edge = jnp.where(tools["first_z"], pltpu.roll(eb[1, c], rp, 0), 0.0)
        edge += jnp.where(tools["last_z"], pltpu.roll(eb[2, c], rows - rp, 0), 0.0)
        own_i[c] = own_i[c] + DIFFUSION * edge
        ix[H, t, c] = own_i[c]
    share(ix, i_send, i_recv, near_order)
    share(ix, i_send, i_recv, far_order, t == 0)

    settle(bx, b_recv, near_order)
    inside = [(s + d >= 0) & (s + d < Z) for d in range(-H, H + 1)]

    def advance(m_fields, reach):
        result = {}
        for d in range(-reach, reach + 1):
            out = coarse_step(plan, tools, m_fields.get(d - 1), m_fields[d], m_fields.get(d + 1))
            result[d] = out if d == 0 else jnp.where(inside[H + d], out, 0.0)
        return result

    prod[...] = jnp.zeros(prod.shape, jnp.float32)

    def powers(m, carry):
        sums_i = [None] * (S - 1)
        sums_b = [None] * (S - 1)
        for c in range(C):
            reach = min(H, -(-(S - 2) // p))
            fields = {d: bx[H + d, m, c] for d in range(-reach, reach + 1)}
            for k in range(S - 1):
                if k > 0:
                    fields = advance(fields, min(H, -(-(S - 2 - k) // p)))
                ti, tb = fields[0] * own_i[c], fields[0] * own_b[c]
                sums_i[k] = ti if c == 0 else sums_i[k] + ti
                sums_b[k] = tb if c == 0 else sums_b[k] + tb
        for k in range(S - 1):
            prod[k * S + m] = jnp.sum(sums_i[k], axis=0, keepdims=True)
            prod[(S - 1 + k) * S + m] = jnp.sum(sums_b[k], axis=0, keepdims=True)
        return carry

    if S <= 4:
        for m in range(S):
            powers(m, 0)
    else:
        lax.fori_loop(0, S, powers, 0)
    message = dot(jnp.ones((8, LANES), jnp.float32), prod[:, 0, :], ((1,), (1,)))
    def tell(buf, index, size, step, device):
        def one(k, carry):
            send(buf.at[index], buf.at[index], m_send.at[step], m_recv.at[step], device(k)).start()
            return carry

        lax.fori_loop(1, size, one, 0)
        view = buf.at[pl.ds(0, size - 1)]
        pltpu.make_async_copy(view, view, m_recv.at[step]).wait()
        return pltpu.make_async_copy(view, view, m_send.at[step])

    mz[s] = message[0:1]
    if plan.SP > S:
        mt[pl.ds(S, plan.SP - S)] = jnp.zeros((plan.SP - S, 1, plan.LQ), jnp.float32)
    told_z = tell(mz, s, Z, 0, lambda k: (t, lax.rem(s + k, Z)))
    mt[t] = jnp.sum(mz[:, 0, :], axis=0, keepdims=True)
    told_t = tell(mt, t, S, 1, lambda k: (lax.rem(t + k, S), s))
    owner = pick(iota((plan.SP, LANES), 0) == iota((plan.SP, LANES), 1))
    table = dot(mt[:, 0, :], owner, ((0,), (0,)))

    def block(kind, k):
        at = (kind * (S - 1) + k) * S
        return table[at : at + S]

    row, lane = iota((S, LANES), 0), iota((S, LANES), 1)
    lane1 = iota((1, LANES), 1)
    swept = block(1, 0)
    for i in range(S):
        pivot_row = swept[i : i + 1]
        pivot_col = jnp.sum(jnp.where(lane == i, swept, 0.0), axis=1, keepdims=True)
        pivot = jnp.sum(jnp.where(lane1 == i, pivot_row, 0.0), axis=1, keepdims=True)
        inv = 1.0 / pivot
        body = swept - pivot_col * (pivot_row * inv)
        body = jnp.where(row == i, pivot_row * inv, body)
        body = jnp.where(lane == i, pivot_col * inv, body)
        swept = jnp.where((row == i) & (lane == i), -inv, body)
    inverse = -swept
    mats = [block(0, k) - block(1, k + 1) for k in range(S - 2)]
    coeffs = []
    for j in range(1, S):
        p_col = jnp.sum(jnp.where(lane == 0, block(0, j - 1), 0.0), axis=1, keepdims=True)
        if j > 1:
            terms = jnp.zeros((S, LANES), jnp.float32)
            for i in range(1, j):
                terms += mats[j - 1 - i] * coeffs[i - 1]
            p_col = p_col + jnp.sum(terms, axis=1, keepdims=True)
        coeffs.append(
            jnp.where(lane1 < S, jnp.sum(inverse * p_col, axis=0, keepdims=True), 0.0)
        )

    at_down(halo_up.wait_recv)
    at_up(halo_down.wait_recv)
    for c in range(C):
        o[c, 0, 0] += far * lo[c, 0] + near * lo[c, 1]
        o[c, 0, 1] += far * lo[c, 1]
        o[c, p - 1, COARSEN - 1] += near * hi[c, 0] + far * hi[c, 1]
        o[c, p - 1, COARSEN - 2] += far * hi[c, 0]
    store_fine = pltpu.make_async_copy(o, fine_hbm, out_sem)
    store_fine.start()
    settle(bx, b_recv, far_order)
    settle(ix, i_recv, near_order)
    settle(ix, i_recv, far_order, 1)

    carried = []
    weights = [
        [jnp.sum(jnp.where(lane1 == m, coeffs[j], 0.0), axis=1, keepdims=True) for m in range(S)]
        for j in range(S - 1)
    ]
    for c in range(C):
        w = {d: ix[H + d, 0, c] for d in range(-H, H + 1)}
        mine = w[0]
        for j in range(1, S):
            reach = min(H, -(-(S - 1 - j) // p))
            source = min(H, reach + 1)
            left = {}
            for d in range(-source, source + 1):
                if d not in w:
                    continue
                value = w[d]
                for m in range(S):
                    value = value - weights[j - 1][m] * bx[H + d, m, c]
                left[d] = value
            moved = advance(left, reach)
            w = {}
            for d in range(-reach, reach + 1):
                value = moved[d]
                for m in range(S):
                    value = value + weights[j - 1][m] * ix[H + d, m, c]
                w[d] = value
            mine = jnp.where(t == j, w[0], mine)
        carried.append(mine - own_i[c])

    for c in range(C):
        stack = jnp.concatenate(
            [jnp.where(group_of == g, carried[c], 0.0) for g in range(groups)], axis=0
        )
        tallc = dot(gather_x, stack, ((0,), (0,)))
        full = dot(tallc, spread_y, ((1,), (1,)))
        for zz in range(p):
            add_ref[c, zz] = full[zz * X : (zz + 1) * X]

    store_fine.wait()
    settle(bx, b_send, near_order + far_order)
    settle(ix, i_send, near_order)
    settle(ix, i_send, far_order, S, t == 0)
    told_z.wait()
    told_t.wait()
    at_up(halo_up.wait_send, edge_up.wait_send)
    at_down(halo_down.wait_send, edge_down.wait_send)


def local(starts, strain):
    slices, slabs = lax.axis_size("tm"), lax.axis_size("space")
    plan = Plan(slices, slabs, starts.shape[1:])
    C, D, X, Y = starts.shape[1:]
    f32 = jnp.float32
    coarse = (plan.W, plan.S, C, plan.rows, LANES)
    dma = pltpu.SemaphoreType.DMA
    fine, add = pl.pallas_call(
        functools.partial(kernel, plan),
        out_shape=(
            jax.ShapeDtypeStruct((C, plan.p, COARSEN, X, Y), f32),
            jax.ShapeDtypeStruct((C, plan.p, X, Y), f32),
        ),
        in_specs=[pl.BlockSpec(memory_space=pl.ANY)] * 2,
        out_specs=(
            pl.BlockSpec(memory_space=pl.ANY),
            pl.BlockSpec(memory_space=pltpu.VMEM),
        ),
        scratch_shapes=[
            pltpu.VMEM((C, D + 4, X, Y), f32),
            pltpu.VMEM(strain.shape[1:], strain.dtype),
            pltpu.VMEM((C, plan.p, COARSEN, X, Y), f32),
            pltpu.VMEM((C, 2, X, Y), f32),
            pltpu.VMEM((C, 2, X, Y), f32),
            pltpu.VMEM((3, C, plan.rows, LANES), f32),
            pltpu.VMEM(coarse, f32),
            pltpu.VMEM(coarse, f32),
            pltpu.VMEM((plan.LQ, 1, LANES), f32),
            pltpu.VMEM((slabs, 1, plan.LQ), f32),
            pltpu.VMEM((plan.SP, 1, plan.LQ), f32),
            dma((2,)), dma(()), dma((2,)), dma((2,)), dma((2,)), dma((2,)),
            dma((plan.W,)), dma((plan.W,)), dma((plan.W,)), dma((plan.W,)),
            dma((2,)), dma((2,)),
        ],
        compiler_params=pltpu.CompilerParams(collective_id=0, has_side_effects=True),
    )(starts, strain)
    return (fine + add[:, :, None]).reshape(1, C, D, X, Y)


def solution(mesh):
    return jax.shard_map(
        local,
        mesh=mesh,
        in_specs=(P("tm", None, "space", None, None), P("tm", None, "space", None, None)),
        out_specs=P("tm", None, "space", None, None),
        check_vma=False,
    )
```

```python
import functools

import jax
import jax.numpy as jnp
from jax import lax
from jax.experimental import pallas as pl
from jax.experimental.pallas import tpu as pltpu
from jax.sharding import PartitionSpec as P

COARSEN = 4
NEAR = 0.8
FAR = 0.2
DIFFUSION = 0.08
RATE = 0.1
LANES = 128
HI = lax.Precision.HIGHEST
MESH = pl.DeviceIdType.MESH


def iota(shape, dim):
    return lax.broadcasted_iota(jnp.int32, shape, dim)


def dot(a, b, dims=((1,), (0,))):
    return lax.dot_general(a, b, (dims, ((), ())), precision=HI, preferred_element_type=jnp.float32)


def pick(condition):
    return jnp.where(condition, 1.0, 0.0).astype(jnp.float32)


class Plan:
    def __init__(self, slices, slabs, block):
        self.S, self.Z = slices, slabs
        self.C, self.D, self.X, self.Y = block
        self.p = self.D // COARSEN
        self.nx, self.ny = self.X // COARSEN, self.Y // COARSEN
        self.groups = LANES // self.ny
        self.rp = self.nx // self.groups
        self.rows = self.p * self.rp
        self.H = min(slabs - 1, -(-(slices - 1) // self.p))
        self.W = 2 * self.H + 1
        self.R = min(self.H, -(-(slices - 2) // self.p))
        self.SP = -(-slices // 8) * 8
        self.count = 2 * (slices - 1) * slices
        self.LQ = -(-self.count // LANES) * LANES


def step_tools(plan):
    shape = (plan.rows, LANES)
    row, lane = iota(shape, 0), iota(shape, 1)
    low = row % plan.rp
    y = lane % plan.ny
    return dict(
        last_y=y == plan.ny - 1,
        first_y=y == 0,
        last_x=low == plan.rp - 1,
        first_x=low == 0,
        last_z=row >= plan.rows - plan.rp,
        first_z=row < plan.rp,
    )


def coarse_step(plan, tools, prev, cur, nxt):
    rows, rp, ny = plan.rows, plan.rp, plan.ny
    roll = pltpu.roll
    total = jnp.where(tools["last_y"], roll(cur, ny - 1, 1), roll(cur, LANES - 1, 1))
    total += jnp.where(tools["first_y"], roll(cur, LANES - ny + 1, 1), roll(cur, 1, 1))
    total += jnp.where(
        tools["last_x"], roll(roll(cur, rp - 1, 0), LANES - ny, 1), roll(cur, rows - 1, 0)
    )
    total += jnp.where(
        tools["first_x"], roll(roll(cur, rows - rp + 1, 0), ny, 1), roll(cur, 1, 0)
    )
    up = roll(cur, rows - rp, 0)
    down = roll(cur, rp, 0)
    zero = jnp.zeros_like(cur)
    above = zero if nxt is None else roll(nxt, rows - rp, 0)
    below = zero if prev is None else roll(prev, rp, 0)
    total += jnp.where(tools["last_z"], above, up) + jnp.where(tools["first_z"], below, down)
    return cur + RATE * (total - 6.0 * cur)


def kernel(
    plan, start_hbm, strain_hbm, o,
    f, st, lo, hi, eb, bx, ix, prod, mz, mt,
    in_sem, halo_send, halo_recv, e_send, e_recv,
    b_send, b_recv, i_send, i_recv, m_send, m_recv,
):
    S, Z, C, D, X, Y, H, R = (
        plan.S, plan.Z, plan.C, plan.D, plan.X, plan.Y, plan.H, plan.R
    )
    p, rows, groups, rp, ny = plan.p, plan.rows, plan.groups, plan.rp, plan.ny
    t, s = lax.axis_index("tm"), lax.axis_index("space")

    load_start = pltpu.make_async_copy(start_hbm.at[0], f.at[:, pl.ds(2, D)], in_sem.at[0])
    load_start.start()
    load_strain = pltpu.make_async_copy(strain_hbm.at[0], st, in_sem.at[1])
    load_strain.start()

    barrier = pltpu.get_barrier_semaphore()

    def greet_slices(slab, first):
        def one(k, carry):
            pl.semaphore_signal(
                barrier, inc=1, device_id=(lax.rem(t + k, S), slab), device_id_type=MESH
            )
            return carry

        lax.fori_loop(first, S, one, 0)

    def greet_slab(slab, carry):
        near = (slab - s <= H) & (s - slab <= H)

        @pl.when(near & (slab != s))
        def _():
            greet_slices(slab, 0)

        @pl.when(jnp.logical_not(near))
        def _():
            pl.semaphore_signal(barrier, inc=1, device_id=(t, slab), device_id_type=MESH)

        return carry

    greet_slices(s, 1)
    lax.fori_loop(0, Z, greet_slab, 0)
    near_slabs = jnp.minimum(s + H, Z - 1) - jnp.maximum(s - H, 0) + 1
    greetings = near_slabs * S - 1 + Z - near_slabs

    spread_y = pick(iota((Y, LANES), 0) // COARSEN == iota((Y, LANES), 1) % ny)
    tall = (groups * rows, p * X)
    a, b = iota(tall, 0), iota(tall, 1)
    coarse_x = (a // rows) * rp + a % rp
    gather_x = pick(((a % rows) // rp == b // X) & ((b % X) // COARSEN == coarse_x))
    group_of = iota((rows, LANES), 1) // ny

    def restrict(plane_sums):
        wide = dot(jnp.concatenate(plane_sums, axis=0), spread_y)
        result = []
        for c in range(len(plane_sums)):
            tallc = dot(gather_x, wide[c * p * X : (c + 1) * p * X])
            total = jnp.zeros((rows, LANES), jnp.float32)
            for g in range(groups):
                total += jnp.where(group_of == g, tallc[g * rows : (g + 1) * rows], 0.0)
            result.append(total * (1.0 / COARSEN**3))
        return result

    load_start.wait()
    sums = []
    for c in range(C):
        planes = []
        for zz in range(p):
            base = 2 + zz * COARSEN
            acc = f[c, base]
            for k in range(1, COARSEN):
                acc = acc + f[c, base + k]
            planes.append(acc)
        sums.append(jnp.concatenate(planes, axis=0))
    for c in range(C):
        bottom = (NEAR + FAR) * f[c, 2] + FAR * f[c, 3]
        top = (NEAR + FAR) * f[c, D + 1] + FAR * f[c, D]
        middle = [jnp.zeros((X, Y), jnp.float32)] * (p - 2)
        sums.append(jnp.concatenate([bottom] + middle + [top], axis=0))
    both = restrict(sums)
    own_b, own_e = both[:C], both[C:]
    for c in range(C):
        bx[H, t, c] = own_b[c]
        eb[0, c] = own_e[c]

    for d in range(-H, H + 1):
        if d != 0:

            @pl.when((s + d < 0) | (s + d >= Z))
            def _():
                bx[H + d] = jnp.zeros((S, C, rows, LANES), jnp.float32)
                ix[H + d] = jnp.zeros((S, C, rows, LANES), jnp.float32)

    f[:, 0:2] = jnp.zeros((C, 2, X, Y), jnp.float32)
    f[:, D + 2 : D + 4] = jnp.zeros((C, 2, X, Y), jnp.float32)

    @pl.when(s == 0)
    def _():
        lo[...] = jnp.zeros((C, 2, X, Y), jnp.float32)
        eb[1] = jnp.zeros((C, rows, LANES), jnp.float32)

    @pl.when(s == Z - 1)
    def _():
        hi[...] = jnp.zeros((C, 2, X, Y), jnp.float32)
        eb[2] = jnp.zeros((C, rows, LANES), jnp.float32)

    pl.semaphore_wait(barrier, greetings)

    above, below = (t, jnp.minimum(s + 1, Z - 1)), (t, jnp.maximum(s - 1, 0))

    def send(src, dst, send_sem, recv_sem, device):
        return pltpu.make_async_remote_copy(
            src_ref=src, dst_ref=dst, send_sem=send_sem, recv_sem=recv_sem,
            device_id=device, device_id_type=MESH,
        )

    halo_up = send(f.at[:, pl.ds(D, 2)], lo, halo_send.at[0], halo_recv.at[0], above)
    halo_down = send(f.at[:, pl.ds(2, 2)], hi, halo_send.at[1], halo_recv.at[1], below)
    edge_up = send(eb.at[0], eb.at[1], e_send.at[0], e_recv.at[0], above)
    edge_down = send(eb.at[0], eb.at[2], e_send.at[1], e_recv.at[1], below)

    def at_up(*actions):
        @pl.when(s < Z - 1)
        def _():
            for action in actions:
                action()

    def at_down(*actions):
        @pl.when(s > 0)
        def _():
            for action in actions:
                action()

    near_order = sorted(range(-R, R + 1), key=abs)
    far_order = [d for d in range(-H, H + 1) if abs(d) > R]

    def share(buf, send_sem, recv_sem, order, condition=True):
        for d in order:

            def one(k, carry):
                send(
                    buf.at[H, t], buf.at[H - d, t], send_sem.at[H + d], recv_sem.at[H - d],
                    (lax.rem(t + k, S), s + d),
                ).start()
                return carry

            @pl.when((s + d >= 0) & (s + d < Z) & condition)
            def _():
                lax.fori_loop(1 if d == 0 else 0, S, one, 0)

    def settle(buf, sem, order, size=S, condition=True):
        for d in order:

            @pl.when((s + d >= 0) & (s + d < Z) & condition)
            def _():
                view = buf.at[H + d, pl.ds(0, size - 1 if d == 0 else size)]
                pltpu.make_async_copy(view, view, sem.at[H + d]).wait()

    at_up(edge_up.start)
    at_down(edge_down.start)
    share(bx, b_send, b_recv, near_order)
    at_up(halo_up.start)
    at_down(halo_down.start)
    load_strain.wait()

    near, far = DIFFUSION * NEAR, DIFFUSION * FAR
    centre = 1.0 - 6.0 * (near + far)

    def fine_plane(z, carry):
        v = [f[c, z + 2] for c in range(C)]
        for c in range(C):
            n1 = f[c, z + 1] + f[c, z + 3]
            n2 = f[c, z] + f[c, z + 4]
            n1 += pltpu.roll(v[c], 1, 0) + pltpu.roll(v[c], X - 1, 0)
            n2 += pltpu.roll(v[c], 2, 0) + pltpu.roll(v[c], X - 2, 0)
            n1 += pltpu.roll(v[c], 1, 1) + pltpu.roll(v[c], Y - 1, 1)
            n2 += pltpu.roll(v[c], 2, 1) + pltpu.roll(v[c], Y - 2, 1)
            acc = centre * v[c] + near * n1 + far * n2
            for j in range(C):
                acc += st[C * c + j, z].astype(jnp.float32) * v[j]
            o[c, z // COARSEN, z % COARSEN] = acc
        return carry

    lax.fori_loop(0, D, fine_plane, 0)
    sums = []
    for c in range(C):
        planes = []
        for zz in range(p):
            acc = o[c, zz, 0]
            for k in range(1, COARSEN):
                acc = acc + o[c, zz, k]
            planes.append(acc)
        sums.append(jnp.concatenate(planes, axis=0))
    own_i = restrict(sums)
    tools = step_tools(plan)
    at_down(edge_up.wait_recv)
    at_up(edge_down.wait_recv)
    for c in range(C):
        edge = jnp.where(tools["first_z"], pltpu.roll(eb[1, c], rp, 0), 0.0)
        edge += jnp.where(tools["last_z"], pltpu.roll(eb[2, c], rows - rp, 0), 0.0)
        own_i[c] = own_i[c] + DIFFUSION * edge
        ix[H, t, c] = own_i[c]

    settle(bx, b_recv, near_order)
    inside = [(s + d >= 0) & (s + d < Z) for d in range(-H, H + 1)]

    def advance(m_fields, reach):
        result = {}
        for d in range(-reach, reach + 1):
            out = coarse_step(plan, tools, m_fields.get(d - 1), m_fields[d], m_fields.get(d + 1))
            result[d] = out if d == 0 else jnp.where(inside[H + d], out, 0.0)
        return result

    prod[...] = jnp.zeros(prod.shape, jnp.float32)

    def powers(m, carry):
        sums_i = [None] * (S - 1)
        sums_b = [None] * (S - 1)
        for c in range(C):
            reach = min(H, -(-(S - 2) // p))
            fields = {d: bx[H + d, m, c] for d in range(-reach, reach + 1)}
            for k in range(S - 1):
                if k > 0:
                    fields = advance(fields, min(H, -(-(S - 2 - k) // p)))
                ti, tb = fields[0] * own_i[c], fields[0] * own_b[c]
                sums_i[k] = ti if c == 0 else sums_i[k] + ti
                sums_b[k] = tb if c == 0 else sums_b[k] + tb
        for k in range(S - 1):
            prod[k * S + m] = jnp.sum(sums_i[k], axis=0, keepdims=True)
            prod[(S - 1 + k) * S + m] = jnp.sum(sums_b[k], axis=0, keepdims=True)
        return carry

    if S <= 4:
        for m in range(S):
            powers(m, 0)
    else:
        lax.fori_loop(0, S, powers, 0)
    message = dot(jnp.ones((8, LANES), jnp.float32), prod[:, 0, :], ((1,), (1,)))
    def tell(buf, index, size, step, device, meanwhile=lambda: None):
        def one(k, carry):
            send(buf.at[index], buf.at[index], m_send.at[step], m_recv.at[step], device(k)).start()
            return carry

        lax.fori_loop(1, size, one, 0)
        meanwhile()
        view = buf.at[pl.ds(0, size - 1)]
        pltpu.make_async_copy(view, view, m_recv.at[step]).wait()
        return pltpu.make_async_copy(view, view, m_send.at[step])

    mz[s] = message[0:1]
    if plan.SP > S:
        mt[pl.ds(S, plan.SP - S)] = jnp.zeros((plan.SP - S, 1, plan.LQ), jnp.float32)

    def bulk():
        share(bx, b_send, b_recv, far_order)
        share(ix, i_send, i_recv, near_order)
        share(ix, i_send, i_recv, far_order, t == 0)

    told_z = tell(mz, s, Z, 0, lambda k: (t, lax.rem(s + k, Z)), bulk)
    mt[t] = jnp.sum(mz[:, 0, :], axis=0, keepdims=True)
    told_t = tell(mt, t, S, 1, lambda k: (lax.rem(t + k, S), s))
    owner = pick(iota((plan.SP, LANES), 0) == iota((plan.SP, LANES), 1))
    table = dot(mt[:, 0, :], owner, ((0,), (0,)))

    def block(kind, k):
        at = (kind * (S - 1) + k) * S
        return table[at : at + S]

    row, lane = iota((S, LANES), 0), iota((S, LANES), 1)
    lane1 = iota((1, LANES), 1)
    swept = block(1, 0)
    for i in range(S):
        pivot_row = swept[i : i + 1]
        pivot_col = jnp.sum(jnp.where(lane == i, swept, 0.0), axis=1, keepdims=True)
        pivot = jnp.sum(jnp.where(lane1 == i, pivot_row, 0.0), axis=1, keepdims=True)
        inv = 1.0 / pivot
        body = swept - pivot_col * (pivot_row * inv)
        body = jnp.where(row == i, pivot_row * inv, body)
        body = jnp.where(lane == i, pivot_col * inv, body)
        swept = jnp.where((row == i) & (lane == i), -inv, body)
    inverse = -swept
    mats = [block(0, k) - block(1, k + 1) for k in range(S - 2)]
    coeffs = []
    for j in range(1, S):
        p_col = jnp.sum(jnp.where(lane == 0, block(0, j - 1), 0.0), axis=1, keepdims=True)
        if j > 1:
            terms = jnp.zeros((S, LANES), jnp.float32)
            for i in range(1, j):
                terms += mats[j - 1 - i] * coeffs[i - 1]
            p_col = p_col + jnp.sum(terms, axis=1, keepdims=True)
        coeffs.append(
            jnp.where(lane1 < S, jnp.sum(inverse * p_col, axis=0, keepdims=True), 0.0)
        )

    at_down(halo_up.wait_recv)
    at_up(halo_down.wait_recv)
    for c in range(C):
        o[c, 0, 0] += far * lo[c, 0] + near * lo[c, 1]
        o[c, 0, 1] += far * lo[c, 1]
        o[c, p - 1, COARSEN - 1] += near * hi[c, 0] + far * hi[c, 1]
        o[c, p - 1, COARSEN - 2] += far * hi[c, 0]
    settle(bx, b_recv, far_order)
    settle(ix, i_recv, near_order)
    settle(ix, i_recv, far_order, 1)

    carried = []
    weights = [
        [jnp.sum(jnp.where(lane1 == m, coeffs[j], 0.0), axis=1, keepdims=True) for m in range(S)]
        for j in range(S - 1)
    ]
    for c in range(C):
        w = {d: ix[H + d, 0, c] for d in range(-H, H + 1)}
        mine = w[0]
        for j in range(1, S):
            reach = min(H, -(-(S - 1 - j) // p))
            source = min(H, reach + 1)
            left = {}
            for d in range(-source, source + 1):
                if d not in w:
                    continue
                value = w[d]
                for m in range(S):
                    value = value - weights[j - 1][m] * bx[H + d, m, c]
                left[d] = value
            moved = advance(left, reach)
            w = {}
            for d in range(-reach, reach + 1):
                value = moved[d]
                for m in range(S):
                    value = value + weights[j - 1][m] * ix[H + d, m, c]
                w[d] = value
            mine = jnp.where(t == j, w[0], mine)
        carried.append(mine - own_i[c])

    for c in range(C):
        stack = jnp.concatenate(
            [jnp.where(group_of == g, carried[c], 0.0) for g in range(groups)], axis=0
        )
        tallc = dot(gather_x, stack, ((0,), (0,)))
        full = dot(tallc, spread_y, ((1,), (1,)))
        for zz in range(p):
            for k in range(COARSEN):
                o[c, zz, k] += full[zz * X : (zz + 1) * X]
    settle(bx, b_send, near_order + far_order)
    settle(ix, i_send, near_order)
    settle(ix, i_send, far_order, S, t == 0)
    told_z.wait()
    told_t.wait()
    at_up(halo_up.wait_send, edge_up.wait_send)
    at_down(halo_down.wait_send, edge_down.wait_send)


def local(starts, strain):
    slices, slabs = lax.axis_size("tm"), lax.axis_size("space")
    plan = Plan(slices, slabs, starts.shape[1:])
    C, D, X, Y = starts.shape[1:]
    f32 = jnp.float32
    coarse = (plan.W, plan.S, C, plan.rows, LANES)
    dma = pltpu.SemaphoreType.DMA
    corrected = pl.pallas_call(
        functools.partial(kernel, plan),
        out_shape=pltpu.VMEM((C, plan.p, COARSEN, X, Y), f32),
        in_specs=[pl.BlockSpec(memory_space=pl.ANY)] * 2,
        out_specs=pl.BlockSpec(memory_space=pltpu.VMEM),
        scratch_shapes=[
            pltpu.VMEM((C, D + 4, X, Y), f32),
            pltpu.VMEM(strain.shape[1:], strain.dtype),
            pltpu.VMEM((C, 2, X, Y), f32),
            pltpu.VMEM((C, 2, X, Y), f32),
            pltpu.VMEM((3, C, plan.rows, LANES), f32),
            pltpu.VMEM(coarse, f32),
            pltpu.VMEM(coarse, f32),
            pltpu.VMEM((plan.LQ, 1, LANES), f32),
            pltpu.VMEM((slabs, 1, plan.LQ), f32),
            pltpu.VMEM((plan.SP, 1, plan.LQ), f32),
            dma((2,)), dma((2,)), dma((2,)), dma((2,)), dma((2,)),
            dma((plan.W,)), dma((plan.W,)), dma((plan.W,)), dma((plan.W,)),
            dma((2,)), dma((2,)),
        ],
        compiler_params=pltpu.CompilerParams(collective_id=0, has_side_effects=True),
    )(starts, strain)
    return corrected.reshape(1, C, D, X, Y)


def solution(mesh):
    return jax.shard_map(
        local,
        mesh=mesh,
        in_specs=(P("tm", None, "space", None, None), P("tm", None, "space", None, None)),
        out_specs=P("tm", None, "space", None, None),
        check_vma=False,
    )
```
